32 devices in a mesh: gx: 8 (over z, x), yz: 4 (over y, core).
Axes of the slice: x: 2, y: 2, z: 4, core: 2. Of those that a mesh axis runs over, the one named last changes fastest.
Arguments:
- velocity: bfloat16 [3, 8, 1024, 2048], P(None, 'gx', None, 'yz'), may hold values from -6 to 6
- mean_flow: float32 [1024], replicated, may hold values from 0.5 to 1.5
- chol_diag: float32 [3, 1024], replicated, may hold values from 0.3 to 3
- chol_off: float32 [3, 1024], replicated, may hold values from -3 to 3
- eddy_x: int32 [1536], replicated, may hold values from -64 to 63
- eddy_y: int32 [1536], replicated, may hold values from 0 to 1023
- eddy_z: int32 [1536], replicated, may hold values from 0 to 2047, as said below
- eddy_signs: int32 [3, 1536], replicated, may hold values from 0 to 1
- tile_lists: int32 [16, 288], P('yz'), may hold values from 0 to 1535, as said below
Outputs:
- velocity_next: bfloat16 [3, 8, 1024, 2048], P(None, 'gx', None, 'yz')
- inflow: float32 [1, 3, 1024, 2048], P(None, None, None, 'yz')
The draws below stay inside these ranges and needn't reach their ends.
Inputs may be any that keep to these rules, and one draw needn't show every extreme that they name: Each tile of 128 spanwise cells is the home of exactly 96 eddies; the home tile of eddy e is eddy_z[e] // 128. `tile_lists`: row t holds, in some order and each once, exactly the eddies whose home tile is t - 1, t or t + 1, counted modulo 16.
All inputs are finite; a program needn't handle non-finite values.
Results may differ from the reference program's by a relative error of at most 0.0047.
Values may be sent and summed in bfloat16 or wider, within the bound.
A program may use at most 192 MiB of HBM per device.

```python
import math
import jax
import jax.numpy as jnp
from jax import lax

NS = 2048
NW = 1024
TILE = 128
STEPS = 1
EPT = 96
SIGMA = 64
TILES = 16
EDDIES = 1536
NX = 8


def eddy_layout(key):
    base = jax.random.fold_in(key, 11)
    key_order, key_offset, key_rows = jax.random.split(base, 3)
    order = jax.random.permutation(key_order, EDDIES).astype(jnp.int32)
    slots = jnp.arange(EDDIES, dtype=jnp.int32)
    home = slots // EPT
    offset = jax.random.randint(key_offset, (EDDIES,), 0, TILE, dtype=jnp.int32)
    centres = jnp.zeros((EDDIES,), jnp.int32).at[order].set(home * TILE + offset)
    tiles = jnp.arange(TILES, dtype=jnp.int32)
    nearby = jnp.stack([(tiles - 1) % TILES, tiles, (tiles + 1) % TILES], axis=1)
    slot_rows = (nearby[:, :, None] * EPT + jnp.arange(EPT, dtype=jnp.int32)[None, None, :]).reshape(TILES, 3 * EPT)
    members = order[slot_rows]
    row_keys = jax.random.split(key_rows, TILES)

    def shuffle_row(row_key, row_values):
        return jax.random.permutation(row_key, row_values)
    shuffled = jax.vmap(shuffle_row)(row_keys, members)
    return (centres, shuffled.astype(jnp.int32))


def draw_eddy_z(key, part):
    centres, listed = eddy_layout(key)
    return centres


def draw_tile_lists(key, part):
    centres, listed = eddy_layout(key)
    return listed


def place_ends(values, rng, low, high):
    shape = values.shape
    index_at = [jax.random.randint(jax.random.fold_in(rng, axis), (), 0, shape[axis]) for axis in range(len(shape))]
    values = values.at[tuple(index_at)].set(low)
    longest = shape.index(max(shape))
    index_at[longest] = (index_at[longest] + 1) % shape[longest]
    return values.at[tuple(index_at)].set(high)


def block_levels(rng, extent, cuts, smallest, top_value):
    gain = 1.0
    for position, blocks in cuts:
        heights = jax.random.uniform(jax.random.fold_in(jax.random.fold_in(rng, 6), position), (blocks,), jnp.float32, smallest / len(cuts), top_value / len(cuts))
        gain = gain * jnp.repeat(jnp.exp(heights), extent[position] // blocks).reshape((-1,) + (1,) * (len(extent) - 1 - position))
    return gain


def noise(rng, extent, deviation, most, cuts=(), held_as=jnp.bfloat16):
    gain = block_levels(rng, extent, cuts, -0.22, 0.18) if cuts else 1.0
    drawn = jax.random.normal(rng, extent, jnp.float32) * deviation * gain
    return jnp.minimum(jnp.maximum(drawn, -most), most).astype(held_as)


def setup_inputs(seed: int = 0) -> dict:
    splits = jax.random.split(jax.random.key(seed), 10)
    return {
        "velocity": noise(splits[0], (3, NX, NW, NS), 1.0, 6.0, ((1, 8), (3, 4))),
        "mean_flow": jnp.clip(jax.random.uniform(splits[1], (NW,), jnp.float32, 0.5, 1.5), 0.5, 1.5),
        "chol_diag": jnp.clip(jnp.exp(jax.random.uniform(splits[2], (3, NW), jnp.float32, math.log(0.3), math.log(3.0))), 0.3, 3.0),
        "chol_off": noise(splits[3], (3, NW), 0.5, 3.0, (), jnp.float32),
        "eddy_x": place_ends(jax.random.randint(splits[4], (EDDIES,), -SIGMA, SIGMA), jax.random.fold_in(splits[4], 1), -SIGMA, SIGMA - 1).astype(jnp.int32),
        "eddy_y": place_ends(jax.random.randint(splits[5], (EDDIES,), 0, NW), jax.random.fold_in(splits[5], 1), 0, NW - 1).astype(jnp.int32),
        "eddy_z": draw_eddy_z(jax.random.fold_in(splits[9], 71), 0),
        "eddy_signs": place_ends(jax.random.randint(splits[7], (3, EDDIES), 0, 2), jax.random.fold_in(splits[7], 1), 0, 1).astype(jnp.int32),
        "tile_lists": draw_tile_lists(jax.random.fold_in(splits[9], 71), 0),
    }


shape_peak = math.sqrt(1.5)
time_step = 0.4
viscosity = 0.3
bulk_speed = 1.0

def tent_shape(ratio):
    return shape_peak * jnp.maximum(0.0, 1.0 - jnp.abs(ratio))

def section_offsets():
    offsets = [float(step_index) for step_index in range(STEPS)]
    return jnp.array(offsets, dtype=jnp.float32) * (bulk_speed * time_step)

def tile_weights(listed_row, tile_index, eddy_x, eddy_y, eddy_z, sign_values, offsets):
    cells_y = jnp.arange(NW, dtype=jnp.int32)
    shape_y = tent_shape((cells_y[None, :] - eddy_y[listed_row][:, None]).astype(jnp.float32) / SIGMA)
    cells_z = tile_index * TILE + jnp.arange(TILE, dtype=jnp.int32)
    offset_z = (cells_z[None, :] - eddy_z[listed_row][:, None] + NS // 2) % NS - NS // 2
    shape_z = tent_shape(offset_z.astype(jnp.float32) / SIGMA)
    shape_x = tent_shape((eddy_x[listed_row].astype(jnp.float32)[None, :] + offsets[:, None]) / SIGMA)
    amplitude = math.sqrt(8.0 * NW / (TILE * EPT))
    weights = amplitude * shape_x[:, None, :, None] * sign_values[:, listed_row][None, :, :, None] * shape_z[None, None]
    return (shape_y.astype(jnp.bfloat16), weights.astype(jnp.bfloat16))

def cosine_basis():
    mode_index = jnp.arange(NW, dtype=jnp.int32)[:, None]
    cell_index = jnp.arange(NW, dtype=jnp.int32)[None, :]
    angles = (mode_index * (2 * cell_index + 1) % (4 * NW)).astype(jnp.float32) * (math.pi / (2 * NW))
    norms = jnp.where(mode_index == 0, math.sqrt(1.0 / NW), math.sqrt(2.0 / NW))
    return norms * jnp.cos(angles)

def cholesky_inlet(fluct, mean_flow, chol_diag, chol_off):
    first = mean_flow[:, None] + chol_diag[0][:, None] * fluct[:, 0]
    second = chol_off[0][:, None] * fluct[:, 0] + chol_diag[1][:, None] * fluct[:, 1]
    third = chol_off[1][:, None] * fluct[:, 0] + chol_off[2][:, None] * fluct[:, 1] + chol_diag[2][:, None] * fluct[:, 2]
    return (first, second, third)

def wall_flux(second):
    keep = (jnp.arange(NW, dtype=jnp.int32) < NW - 1).astype(jnp.float32)[:, None]
    return second * keep

def eigen_scale(mode_y, mode_z):
    rise_y = 2.0 - 2.0 * jnp.cos(mode_y.astype(jnp.float32) * (math.pi / NW))
    rise_z = 2.0 - 2.0 * jnp.cos(mode_z.astype(jnp.float32) * (2.0 * math.pi / NS))
    eigen_sum = -(rise_y + rise_z)
    mean_mode = (mode_y == 0) & (mode_z == 0)
    return jnp.where(mean_mode, 0.0, 1.0 / jnp.where(mean_mode, -1.0, eigen_sum))

def tendency(field, inlet_plane, mean_flow):
    behind = jnp.concatenate([inlet_plane[:, None], field[:, :-1]], axis=1)
    behind = lax.optimization_barrier(behind.astype(jnp.bfloat16)).astype(jnp.float32)
    edge = jnp.zeros_like(field[:, :, :1])
    above = jnp.concatenate([field[:, :, 1:], edge], axis=2)
    below = jnp.concatenate([edge, field[:, :, :-1]], axis=2)
    return -mean_flow[:, None] * (field - behind) - 0.5 * field[1] * (above - below) + viscosity * (above - 2.0 * field + below)

def march(field, inflow, mean_flow):
    for step_index in range(STEPS):
        plane = inflow[step_index]
        first_rate = tendency(field, plane, mean_flow)
        section_one = field + time_step * (8.0 / 15.0) * first_rate
        second_rate = tendency(section_one, plane, mean_flow)
        section_two = section_one + time_step * (5.0 / 12.0 * second_rate - 17.0 / 60.0 * first_rate)
        third_rate = tendency(section_two, plane, mean_flow)
        field = section_two + time_step * (0.75 * third_rate - 5.0 / 12.0 * second_rate)
    return field

def reference(velocity, mean_flow, chol_diag, chol_off, eddy_x, eddy_y, eddy_z, eddy_signs, tile_lists):
    offsets = section_offsets()
    sign_values = (2 * eddy_signs - 1).astype(jnp.float32)

    def one_tile(packed):
        listed_row, tile_index = packed
        shape_y, weights = tile_weights(listed_row, tile_index, eddy_x, eddy_y, eddy_z, sign_values, offsets)
        return jnp.einsum('ly,njlz->njyz', shape_y.astype(jnp.float32), weights.astype(jnp.float32))
    per_tile = lax.map(one_tile, (tile_lists, jnp.arange(TILES, dtype=jnp.int32)))
    fluct = jnp.moveaxis(per_tile, 0, 3).reshape(STEPS, 3, NW, NS)
    first, second, third = cholesky_inlet(fluct, mean_flow, chol_diag, chol_off)
    basis = cosine_basis()
    flux = wall_flux(second)
    lower = jnp.concatenate([jnp.zeros_like(flux[:, :1]), flux[:, :-1]], axis=1)
    div = flux - lower + third - jnp.roll(third, 1, axis=2)
    high = lax.Precision.HIGHEST
    div_modes = jnp.einsum('ky,nyz->nkz', basis, div, precision=high)
    spectrum = jnp.fft.fft(div_modes, axis=2)
    scale = eigen_scale(jnp.arange(NW, dtype=jnp.int32)[:, None], jnp.arange(NS, dtype=jnp.int32)[None, :])
    potential_modes = jnp.real(jnp.fft.ifft(spectrum * scale, axis=2)).astype(jnp.float32)
    potential = jnp.einsum('ky,nkz->nyz', basis, potential_modes, precision=high)
    slope_z = jnp.roll(potential, -1, axis=2) - potential
    rise = jnp.concatenate([potential[:, 1:] - potential[:, :-1], jnp.zeros_like(potential[:, :1])], axis=1)
    inflow = jnp.stack([first, flux - rise, third - slope_z], axis=1)

    def one_block(tile_index):
        start = (tile_index * TILE).astype(jnp.int32)
        block = lax.dynamic_slice_in_dim(velocity, start, TILE, 3).astype(jnp.float32)
        plane = lax.dynamic_slice_in_dim(inflow, start, TILE, 3)
        return march(block, plane, mean_flow).astype(jnp.bfloat16)
    marched = lax.map(one_block, jnp.arange(TILES, dtype=jnp.int32))
    velocity_next = marched.transpose(1, 2, 3, 0, 4).reshape(3, NX, NW, NS)
    return (velocity_next, inflow)
```

```python
import math

import jax
import jax.numpy as jnp
import numpy as np
from jax import lax
from jax.experimental import pallas as pl
from jax.experimental.pallas import tpu as pltpu
from jax.sharding import PartitionSpec as P

TILE = 128
EPT = 96
SIGMA = 64
LANES = 128
WINDOW = 128
HALO = 16

shape_peak = math.sqrt(1.5)
time_step = 0.4
viscosity = 0.3
bulk_speed = 1.0


def tent_shape(ratio):
    return shape_peak * jnp.maximum(0.0, 1.0 - jnp.abs(ratio))


def wall_bases(rows):
    inner = 32
    norm = math.sqrt(2.0 / rows)
    y = np.arange(rows)[None, :]
    p = np.arange(rows // inner)[:, None] * inner
    q = np.arange(inner)[:, None]

    def angles(k, position, period):
        return (k * position % period) * (2.0 * math.pi / period)

    def single(table):
        return jnp.asarray(table.astype(np.float32))

    a, b = angles(p, 2 * y + 1, 4 * rows), angles(q, 2 * y + 1, 4 * rows)
    cosine = (
        single(norm * np.cos(a))[:, None] * single(np.cos(b))[None]
        - single(norm * np.sin(a))[:, None] * single(np.sin(b))[None]
    ).reshape(rows, rows)
    cosine = jnp.where(jnp.arange(rows)[:, None] == 0, math.sqrt(1.0 / rows), cosine)
    a, b = angles(p, y + 1, 2 * rows), angles(q, y + 1, 2 * rows)
    sine = (
        single(norm * np.sin(a))[:, None] * single(np.cos(b))[None]
        + single(norm * np.cos(a))[:, None] * single(np.sin(b))[None]
    ).reshape(rows, rows)
    return cosine, sine


def decay_rates(rows):
    return 2.0 * np.arcsinh(np.sin(np.arange(rows) * (math.pi / (2 * rows))))


def line_kernel(f_ref, coef_ref, g_ref, h_ref):
    rate, alpha, beta = coef_ref[0], coef_ref[1], coef_ref[2]
    mean, carry_up, carry_down = coef_ref[3], coef_ref[4], coef_ref[5]
    length = f_ref.shape[0]

    def down(step, carry):
        z = length - 1 - step
        g_ref[z] = carry
        return f_ref[z] - mean + rate * carry

    lax.fori_loop(0, length, down, carry_down, unroll=8)

    def up(z, carry):
        total = f_ref[z] - mean + rate * carry
        after = g_ref[z]
        g_ref[z] = alpha * (total - after)
        h_ref[z] = beta * (total + rate * after)
        return total

    lax.fori_loop(0, length, up, carry_up, unroll=8)


def line_solve(modes, theta, axis):
    length, rows = modes.shape
    count = lax.axis_size(axis)
    total = count * length
    me = lax.axis_index(axis)
    z = jnp.arange(length, dtype=jnp.float32)[:, None]
    theta_row = jnp.asarray(theta.astype(np.float32))[None]
    weight_up = jnp.exp(-theta_row * (length - 1 - z))
    weight_down = jnp.where(jnp.arange(rows)[None] == 0, length - z, jnp.exp(-theta_row * z))
    sums = jnp.stack([jnp.sum(modes * weight_up, axis=0), jnp.sum(modes * weight_down, axis=0)])
    everyone = lax.all_gather(sums, axis)
    place = jnp.arange(count)
    behind = (me - 1 - place) % count
    ahead = (place - me - 1) % count
    theta_line = jnp.asarray((theta * length).astype(np.float32))
    period = jnp.asarray(np.where(theta > 0, 1.0 / np.maximum(-np.expm1(-theta * total), 1e-30), 1.0).astype(np.float32))
    carry_up = period * jnp.sum(everyone[:, 0] * jnp.exp(-theta_line[None] * behind[:, None].astype(jnp.float32)), axis=0)
    carry_down = period * jnp.sum(everyone[:, 1] * jnp.exp(-theta_line[None] * ahead[:, None].astype(jnp.float32)), axis=0)
    first_tot = everyone[:, 0, 0]
    first_run = everyone[:, 1, 0]
    mean = jnp.sum(first_tot) / total
    tot = first_tot - mean * length
    starts = jnp.cumsum(tot) - tot
    shift = -(jnp.sum(first_run - mean * (length * (length + 1) / 2.0)) + length * jnp.sum(starts)) / total
    mine = (place == me).astype(jnp.float32)
    start = jnp.sum(starts * mine) + shift
    is_first = jnp.arange(rows) == 0
    carry_up = jnp.where(is_first, start, carry_up)
    carry_down = jnp.where(is_first, -start - jnp.sum(tot * mine), carry_down)
    means = jnp.where(is_first, mean, 0.0)
    rate = np.exp(-theta)
    fixed = np.stack([rate, rate / (1.0 + rate), np.sqrt(rate) / (1.0 + rate)]).astype(np.float32)
    coef = jnp.concatenate([jnp.asarray(fixed), jnp.stack([means, carry_up, carry_down])], axis=0)
    lanes = (rows // LANES, LANES)
    g, h = pl.pallas_call(
        line_kernel,
        out_shape=[jax.ShapeDtypeStruct((length,) + lanes, jnp.float32)] * 2,
        in_specs=[pl.BlockSpec(memory_space=pltpu.VMEM)] * 2,
        out_specs=[pl.BlockSpec(memory_space=pltpu.VMEM)] * 2,
        compiler_params=pltpu.CompilerParams(vmem_limit_bytes=24 * 1024 * 1024),
        cost_estimate=pl.CostEstimate(
            flops=10 * length * rows, bytes_accessed=12 * length * rows, transcendentals=0
        ),
        name="line_solve",
    )(modes.reshape((length,) + lanes), coef.reshape((6,) + lanes))
    return g.reshape(length, rows), h.reshape(length, rows)


def march_kernel(level_ref, mean_ref, inlet_ref, far_ref, q0_ref, q1_ref, p0_ref, p1_ref, o0_ref, o1_ref):
    rows = mean_ref.shape[0]
    level = level_ref[0]
    at_inlet = level == 0
    after_inlet = level == 1
    stride = WINDOW - 2 * HALO
    count = -(-(rows - WINDOW) // stride) + 1
    local = lax.broadcasted_iota(jnp.int32, (WINDOW, LANES), 0)

    def window(index, carry):
        start = pl.multiple_of(jnp.minimum(index * stride, rows - WINDOW), HALO)
        here = pl.ds(start, WINDOW)
        low_wall = local + start == 0
        high_wall = local + start == rows - 1
        mean = mean_ref[here, :]
        drag = mean + 2.0 * viscosity

        def load(ref):
            return [ref[c, here, :].astype(jnp.float32) for c in range(3)]

        def rate(field, behind):
            half = 0.5 * field[1]
            up, down = viscosity - half, viscosity + half
            out = []
            for c in range(3):
                above = jnp.where(high_wall, 0.0, jnp.roll(field[c], -1, axis=0))
                below = jnp.where(low_wall, 0.0, jnp.roll(field[c], 1, axis=0))
                out.append(up * above + down * below + mean * behind[c] - drag * field[c])
            return out

        def pick(flag, first, second):
            return [jnp.where(flag, a, b) for a, b in zip(first, second)]

        def rounded(field):
            return [a.astype(jnp.bfloat16).astype(jnp.float32) for a in field]

        def one(field, f0):
            return [u + time_step * (8.0 / 15.0) * a for u, a in zip(field, f0)]

        def two(field, f1, f0):
            return [
                u + (time_step * 5.0 / 12.0) * b - (time_step * 17.0 / 60.0) * a
                for u, b, a in zip(field, f1, f0)
            ]

        def three(field, f2, f1):
            return [
                u + (time_step * 0.75) * b - (time_step * 5.0 / 12.0) * a
                for u, b, a in zip(field, f2, f1)
            ]

        inlet = load(inlet_ref)
        far = pick(after_inlet, inlet, load(far_ref))
        q0, q1, p0, p1 = load(q0_ref), load(q1_ref), load(p0_ref), load(p1_ref)
        q0_1 = rounded(one(q0, rate(q0, far)))
        q1_f0 = rate(q1, q0)
        q1_1 = one(q1, q1_f0)
        q1_2 = rounded(two(q1_1, rate(q1_1, q0_1), q1_f0))
        p0_f0 = rate(p0, pick(at_inlet, inlet, q1))
        p0_1 = one(p0, p0_f0)
        p0_f1 = rate(p0_1, pick(at_inlet, inlet, rounded(q1_1)))
        p0_2 = two(p0_1, p0_f1, p0_f0)
        p0_3 = three(p0_2, rate(p0_2, pick(at_inlet, inlet, q1_2)), p0_f1)
        p1_f0 = rate(p1, p0)
        p1_1 = one(p1, p1_f0)
        p1_f1 = rate(p1_1, rounded(p0_1))
        p1_2 = two(p1_1, p1_f1, p1_f0)
        p1_3 = three(p1_2, rate(p1_2, rounded(p0_2)), p1_f1)
        inner = pl.ds(pl.multiple_of(start + HALO, HALO), WINDOW - HALO)
        results = ((o0_ref, p0_3), (o1_ref, p1_3))
        for ref, value in results:
            for c in range(3):
                ref[c, inner, :] = value[c][HALO:].astype(ref.dtype)

        @pl.when(index == 0)
        def _():
            for ref, value in results:
                for c in range(3):
                    ref[c, 0:HALO, :] = value[c][:HALO].astype(ref.dtype)

        return carry

    lax.fori_loop(0, count, window, 0)


def march(level, mean_lanes, inlet, far, q0, q1, p0, p1):
    shape = p0.shape
    rows = shape[1]
    flops = 9 * 3 * 12 * rows * LANES
    return pl.pallas_call(
        march_kernel,
        out_shape=[jax.ShapeDtypeStruct(shape, jnp.bfloat16)] * 2,
        in_specs=[pl.BlockSpec(memory_space=pltpu.SMEM)] + [pl.BlockSpec(memory_space=pltpu.VMEM)] * 7,
        out_specs=[pl.BlockSpec(memory_space=pltpu.VMEM)] * 2,
        compiler_params=pltpu.CompilerParams(vmem_limit_bytes=28 * 1024 * 1024),
        cost_estimate=pl.CostEstimate(flops=flops, bytes_accessed=16 * 3 * rows * LANES, transcendentals=0),
        name="march",
    )(level, mean_lanes, inlet, far, q0, q1, p0, p1)


def inlet_planes(mean_flow, chol_diag, chol_off, eddy_x, eddy_y, eddy_z, eddy_signs, columns, spanwise):
    rows = mean_flow.shape[0]
    first_cell = lax.axis_index("yz") * columns
    signs = (2 * eddy_signs - 1).astype(jnp.float32)
    cells_y = jnp.arange(rows, dtype=jnp.int32)
    shape_y = tent_shape((cells_y[None, :] - eddy_y[:, None]).astype(jnp.float32) / SIGMA).astype(jnp.bfloat16)
    amplitude = math.sqrt(8.0 * rows / (TILE * EPT))
    scale = (amplitude * tent_shape(eddy_x.astype(jnp.float32) / SIGMA))[None, :] * signs

    def fluct_at(cells):
        offset = (cells[None, :] - eddy_z[:, None] + spanwise // 2) % spanwise - spanwise // 2
        shape_z = tent_shape(offset.astype(jnp.float32) / SIGMA)
        weight = (scale[:, :, None] * shape_z[None]).astype(jnp.bfloat16)
        return jnp.einsum("ey,jez->jyz", shape_y, weight, preferred_element_type=jnp.float32)

    fluct = fluct_at(first_cell + jnp.arange(columns, dtype=jnp.int32))
    edge = fluct_at((first_cell - 1 + spanwise) % spanwise + jnp.arange(1, dtype=jnp.int32))

    def mix(fl):
        return chol_off[1][:, None] * fl[0] + chol_off[2][:, None] * fl[1] + chol_diag[2][:, None] * fl[2]

    first = mean_flow[:, None] + chol_diag[0][:, None] * fluct[0]
    second = chol_off[0][:, None] * fluct[0] + chol_diag[1][:, None] * fluct[1]
    third = mix(fluct)
    flux = second * (cells_y < rows - 1).astype(jnp.float32)[:, None]
    lower = jnp.concatenate([jnp.zeros_like(flux[:1]), flux[:-1]], axis=0)
    previous = jnp.concatenate([mix(edge), third[:, :-1]], axis=1)
    div = flux - lower + third - previous
    high = lax.Precision.HIGH
    cosine, sine = wall_bases(rows)
    modes = jnp.einsum("yz,ky->zk", div, cosine, precision=high)
    slope_modes, rise_modes = line_solve(modes, decay_rates(rows), "yz")
    slope = jnp.einsum("ky,zk->yz", cosine, slope_modes, precision=high)
    rise = jnp.einsum("ky,zk->yz", sine, rise_modes, precision=high)
    return jnp.stack([first, flux - rise, third - slope], axis=0)


def body(velocity, mean_flow, chol_diag, chol_off, eddy_x, eddy_y, eddy_z, eddy_signs, tile_lists):
    rows, columns = velocity.shape[2:]
    spanwise = columns * lax.axis_size("yz")
    slabs = lax.axis_size("gx")
    plane = velocity[:, 0]
    me = lax.axis_index("gx")
    even = me % 2 == 0
    half = columns // 2
    swap = [(i, i ^ 1) for i in range(slabs)]
    onward = [(i, i + 2) for i in range(slabs - 2)]
    chunks = []
    for begin in range(0, half, LANES):
        low = plane[:, :, begin : begin + LANES]
        high = plane[:, :, half + begin : half + begin + LANES]
        keep = jnp.where(even, low, high)
        other = lax.ppermute(jnp.where(even, high, low), "gx", swap)
        p0 = jnp.where(even, keep, other)
        p1 = jnp.where(even, other, keep)
        q1 = lax.ppermute(p1, "gx", onward)
        q0 = lax.ppermute(p0, "gx", onward)
        far = lax.ppermute(q1, "gx", onward)
        chunks.append((far, q0, q1, p0, p1))

    inflow = inlet_planes(
        mean_flow, chol_diag, chol_off, eddy_x, eddy_y, eddy_z, eddy_signs, columns, spanwise
    )
    mean_lanes = jnp.broadcast_to(mean_flow[:, None], (rows, LANES))
    level = (me // 2).astype(jnp.int32).reshape(1)
    lows, highs = [], []
    for number, planes in enumerate(chunks):
        begin = number * LANES
        inlet = jnp.where(
            even, inflow[:, :, begin : begin + LANES], inflow[:, :, half + begin : half + begin + LANES]
        ).astype(jnp.bfloat16)
        o0, o1 = march(level, mean_lanes, inlet, *planes)
        keep = jnp.where(even, o0, o1)
        other = lax.ppermute(jnp.where(even, o1, o0), "gx", swap)
        lows.append(jnp.where(even, keep, other))
        highs.append(jnp.where(even, other, keep))
    velocity_next = jnp.concatenate(lows + highs, axis=2)[:, None]
    return (velocity_next, inflow[None])


def solution(mesh):
    placed = (P(None, "gx", None, "yz"), P(), P(), P(), P(), P(), P(), P(), P("yz", None))
    return jax.shard_map(
        body,
        mesh=mesh,
        in_specs=placed,
        out_specs=(P(None, "gx", None, "yz"), P(None, None, None, "yz")),
        check_vma=False,
    )
```

```python
import math

import jax
import jax.numpy as jnp
import numpy as np
from jax import lax
from jax.experimental import pallas as pl
from jax.experimental.pallas import tpu as pltpu
from jax.sharding import PartitionSpec as P

TILE = 128
EPT = 96
SIGMA = 64
LANES = 128
WINDOW = 128
HALO = 16

shape_peak = math.sqrt(1.5)
time_step = 0.4
viscosity = 0.3
bulk_speed = 1.0


def tent_shape(ratio):
    return shape_peak * jnp.maximum(0.0, 1.0 - jnp.abs(ratio))


def wall_bases(rows):
    inner = 32
    norm = math.sqrt(2.0 / rows)
    y = np.arange(rows)[None, :]
    p = np.arange(rows // inner)[:, None] * inner
    q = np.arange(inner)[:, None]

    def angles(k, position, period):
        return (k * position % period) * (2.0 * math.pi / period)

    def single(table):
        return jnp.asarray(table.astype(np.float32))

    a, b = angles(p, 2 * y + 1, 4 * rows), angles(q, 2 * y + 1, 4 * rows)
    cosine = (
        single(norm * np.cos(a))[:, None] * single(np.cos(b))[None]
        - single(norm * np.sin(a))[:, None] * single(np.sin(b))[None]
    ).reshape(rows, rows)
    cosine = jnp.where(jnp.arange(rows)[:, None] == 0, math.sqrt(1.0 / rows), cosine)
    a, b = angles(p, y + 1, 2 * rows), angles(q, y + 1, 2 * rows)
    sine = (
        single(norm * np.sin(a))[:, None] * single(np.cos(b))[None]
        + single(norm * np.cos(a))[:, None] * single(np.sin(b))[None]
    ).reshape(rows, rows)
    return cosine, sine


def decay_rates(rows):
    return 2.0 * np.arcsinh(np.sin(np.arange(rows) * (math.pi / (2 * rows))))


def line_kernel(f_ref, coef_ref, g_ref, h_ref):
    rate, alpha, beta = coef_ref[0], coef_ref[1], coef_ref[2]
    mean, carry_up, carry_down = coef_ref[3], coef_ref[4], coef_ref[5]
    length = f_ref.shape[0]

    def down(step, carry):
        z = length - 1 - step
        g_ref[z] = carry
        return f_ref[z] - mean + rate * carry

    lax.fori_loop(0, length, down, carry_down, unroll=8)

    def up(z, carry):
        total = f_ref[z] - mean + rate * carry
        after = g_ref[z]
        g_ref[z] = alpha * (total - after)
        h_ref[z] = beta * (total + rate * after)
        return total

    lax.fori_loop(0, length, up, carry_up, unroll=8)


def line_solve(modes, theta, axis, held, forward):
    length, rows = modes.shape
    count = lax.axis_size(axis)
    total = count * length
    me = lax.axis_index(axis)
    short = 32
    outer = np.arange(length // short)[:, None]
    inner = np.arange(short)[:, None]
    blocks = modes.reshape(length // short, short, rows)
    up_out = np.exp(-theta[None] * (length - short - short * outer))
    up_in = np.exp(-theta[None] * (short - 1 - inner))
    down_out = np.exp(-theta[None] * short * outer)
    down_in = np.exp(-theta[None] * inner)
    down_in[:, 0] = inner[:, 0]
    down_out[:, 0] = -1.0
    extra = np.zeros_like(up_out)
    extra[:, 0] = length - short * outer[:, 0]
    table = lambda values: jnp.asarray(values.astype(np.float32))
    part_up = jnp.sum(blocks * table(up_in)[None], axis=1)
    part_down = jnp.sum(blocks * table(down_in)[None], axis=1)
    sums = jnp.stack(
        [
            jnp.sum(part_up * table(up_out), axis=0),
            jnp.sum(part_down * table(down_out) + part_up * table(extra), axis=0),
        ]
    )
    sums, held = lax.optimization_barrier((sums, held))
    onward = forward(held)
    everyone = lax.all_gather(sums, axis)
    place = jnp.arange(count)
    behind = (me - 1 - place) % count
    ahead = (place - me - 1) % count
    theta_line = jnp.asarray((theta * length).astype(np.float32))
    period = jnp.asarray(np.where(theta > 0, 1.0 / np.maximum(-np.expm1(-theta * total), 1e-30), 1.0).astype(np.float32))
    carry_up = period * jnp.sum(everyone[:, 0] * jnp.exp(-theta_line[None] * behind[:, None].astype(jnp.float32)), axis=0)
    carry_down = period * jnp.sum(everyone[:, 1] * jnp.exp(-theta_line[None] * ahead[:, None].astype(jnp.float32)), axis=0)
    first_tot = everyone[:, 0, 0]
    first_run = everyone[:, 1, 0]
    mean = jnp.sum(first_tot) / total
    tot = first_tot - mean * length
    starts = jnp.cumsum(tot) - tot
    shift = -(jnp.sum(first_run - mean * (length * (length + 1) / 2.0)) + length * jnp.sum(starts)) / total
    mine = (place == me).astype(jnp.float32)
    start = jnp.sum(starts * mine) + shift
    is_first = jnp.arange(rows) == 0
    carry_up = jnp.where(is_first, start, carry_up)
    carry_down = jnp.where(is_first, -start - jnp.sum(tot * mine), carry_down)
    means = jnp.where(is_first, mean, 0.0)
    rate = np.exp(-theta)
    fixed = np.stack([rate, rate / (1.0 + rate), np.sqrt(rate) / (1.0 + rate)]).astype(np.float32)
    coef = jnp.concatenate([jnp.asarray(fixed), jnp.stack([means, carry_up, carry_down])], axis=0)
    lanes = (rows // LANES, LANES)
    g, h = pl.pallas_call(
        line_kernel,
        out_shape=[jax.ShapeDtypeStruct((length,) + lanes, jnp.float32)] * 2,
        in_specs=[pl.BlockSpec(memory_space=pltpu.VMEM)] * 2,
        out_specs=[pl.BlockSpec(memory_space=pltpu.VMEM)] * 2,
        compiler_params=pltpu.CompilerParams(vmem_limit_bytes=24 * 1024 * 1024),
        cost_estimate=pl.CostEstimate(
            flops=10 * length * rows, bytes_accessed=12 * length * rows, transcendentals=0
        ),
        name="line_solve",
    )(modes.reshape((length,) + lanes), coef.reshape((6,) + lanes))
    return g.reshape(length, rows), h.reshape(length, rows), held, onward


def march_kernel(level_ref, mean_ref, inlet_ref, far_ref, q0_ref, q1_ref, p0_ref, p1_ref, o0_ref, o1_ref):
    rows = mean_ref.shape[0]
    level = level_ref[0]
    at_inlet = level == 0
    after_inlet = level == 1
    stride = WINDOW - 2 * HALO
    count = -(-(rows - WINDOW) // stride) + 1
    local = lax.broadcasted_iota(jnp.int32, (WINDOW, LANES), 0)

    def window(index, carry):
        start = pl.multiple_of(jnp.minimum(index * stride, rows - WINDOW), HALO)
        here = pl.ds(start, WINDOW)
        low_wall = local + start == 0
        high_wall = local + start == rows - 1
        mean = mean_ref[here, :]
        drag = mean + 2.0 * viscosity

        def load(ref):
            return [ref[c, here, :].astype(jnp.float32) for c in range(3)]

        def rate(field, behind):
            half = 0.5 * field[1]
            up, down = viscosity - half, viscosity + half
            out = []
            for c in range(3):
                above = jnp.where(high_wall, 0.0, jnp.roll(field[c], -1, axis=0))
                below = jnp.where(low_wall, 0.0, jnp.roll(field[c], 1, axis=0))
                out.append(up * above + down * below + mean * behind[c] - drag * field[c])
            return out

        def pick(flag, first, second):
            return [jnp.where(flag, a, b) for a, b in zip(first, second)]

        def rounded(field):
            return [a.astype(jnp.bfloat16).astype(jnp.float32) for a in field]

        def one(field, f0):
            return [u + time_step * (8.0 / 15.0) * a for u, a in zip(field, f0)]

        def two(field, f1, f0):
            return [
                u + (time_step * 5.0 / 12.0) * b - (time_step * 17.0 / 60.0) * a
                for u, b, a in zip(field, f1, f0)
            ]

        def three(field, f2, f1):
            return [
                u + (time_step * 0.75) * b - (time_step * 5.0 / 12.0) * a
                for u, b, a in zip(field, f2, f1)
            ]

        inlet = load(inlet_ref)
        far = pick(after_inlet, inlet, load(far_ref))
        q0, q1, p0, p1 = load(q0_ref), load(q1_ref), load(p0_ref), load(p1_ref)
        q0_1 = rounded(one(q0, rate(q0, far)))
        q1_f0 = rate(q1, q0)
        q1_1 = one(q1, q1_f0)
        q1_2 = rounded(two(q1_1, rate(q1_1, q0_1), q1_f0))
        p0_f0 = rate(p0, pick(at_inlet, inlet, q1))
        p0_1 = one(p0, p0_f0)
        p0_f1 = rate(p0_1, pick(at_inlet, inlet, rounded(q1_1)))
        p0_2 = two(p0_1, p0_f1, p0_f0)
        p0_3 = three(p0_2, rate(p0_2, pick(at_inlet, inlet, q1_2)), p0_f1)
        p1_f0 = rate(p1, p0)
        p1_1 = one(p1, p1_f0)
        p1_f1 = rate(p1_1, rounded(p0_1))
        p1_2 = two(p1_1, p1_f1, p1_f0)
        p1_3 = three(p1_2, rate(p1_2, rounded(p0_2)), p1_f1)
        inner = pl.ds(pl.multiple_of(start + HALO, HALO), WINDOW - HALO)
        results = ((o0_ref, p0_3), (o1_ref, p1_3))
        for ref, value in results:
            for c in range(3):
                ref[c, inner, :] = value[c][HALO:].astype(ref.dtype)

        @pl.when(index == 0)
        def _():
            for ref, value in results:
                for c in range(3):
                    ref[c, 0:HALO, :] = value[c][:HALO].astype(ref.dtype)

        return carry

    lax.fori_loop(0, count, window, 0)


def march(level, mean_lanes, inlet, far, q0, q1, p0, p1):
    shape = p0.shape
    rows = shape[1]
    flops = 9 * 3 * 12 * rows * LANES
    return pl.pallas_call(
        march_kernel,
        out_shape=[jax.ShapeDtypeStruct(shape, jnp.bfloat16)] * 2,
        in_specs=[pl.BlockSpec(memory_space=pltpu.SMEM)] + [pl.BlockSpec(memory_space=pltpu.VMEM)] * 7,
        out_specs=[pl.BlockSpec(memory_space=pltpu.VMEM)] * 2,
        compiler_params=pltpu.CompilerParams(vmem_limit_bytes=28 * 1024 * 1024),
        cost_estimate=pl.CostEstimate(flops=flops, bytes_accessed=16 * 3 * rows * LANES, transcendentals=0),
        name="march",
    )(level, mean_lanes, inlet, far, q0, q1, p0, p1)


def inlet_planes(mean_flow, chol_diag, chol_off, eddy_x, eddy_y, eddy_z, eddy_signs, columns, spanwise, held, forward):
    rows = mean_flow.shape[0]
    first_cell = lax.axis_index("yz") * columns
    signs = (2 * eddy_signs - 1).astype(jnp.float32)
    cells_y = jnp.arange(rows, dtype=jnp.int32)
    shape_y = tent_shape((cells_y[None, :] - eddy_y[:, None]).astype(jnp.float32) / SIGMA).astype(jnp.bfloat16)
    amplitude = math.sqrt(8.0 * rows / (TILE * EPT))
    scale = (amplitude * tent_shape(eddy_x.astype(jnp.float32) / SIGMA))[None, :] * signs

    def fluct_at(cells):
        offset = (cells[None, :] - eddy_z[:, None] + spanwise // 2) % spanwise - spanwise // 2
        shape_z = tent_shape(offset.astype(jnp.float32) / SIGMA)
        weight = (scale[:, :, None] * shape_z[None]).astype(jnp.bfloat16)
        return jnp.einsum("ey,jez->jyz", shape_y, weight, preferred_element_type=jnp.float32)

    fluct = fluct_at(first_cell + jnp.arange(columns, dtype=jnp.int32))
    edge = fluct_at((first_cell - 1 + spanwise) % spanwise + jnp.arange(1, dtype=jnp.int32))

    def mix(fl):
        return chol_off[1][:, None] * fl[0] + chol_off[2][:, None] * fl[1] + chol_diag[2][:, None] * fl[2]

    first = mean_flow[:, None] + chol_diag[0][:, None] * fluct[0]
    second = chol_off[0][:, None] * fluct[0] + chol_diag[1][:, None] * fluct[1]
    third = mix(fluct)
    flux = second * (cells_y < rows - 1).astype(jnp.float32)[:, None]
    lower = jnp.concatenate([jnp.zeros_like(flux[:1]), flux[:-1]], axis=0)
    previous = jnp.concatenate([mix(edge), third[:, :-1]], axis=1)
    div = flux - lower + third - previous
    high = lax.Precision.HIGH
    cosine, sine = wall_bases(rows)
    modes = jnp.einsum("yz,ky->zk", div, cosine, precision=high)
    slope_modes, rise_modes, held, onward = line_solve(modes, decay_rates(rows), "yz", held, forward)
    slope = jnp.einsum(
        "ky,zk->yz", cosine.astype(jnp.bfloat16), slope_modes.astype(jnp.bfloat16), preferred_element_type=jnp.float32
    )
    rise = jnp.einsum(
        "ky,zk->yz", sine.astype(jnp.bfloat16), rise_modes.astype(jnp.bfloat16), preferred_element_type=jnp.float32
    )
    return jnp.stack([first, flux - rise, third - slope], axis=0), held, onward


def body(velocity, mean_flow, chol_diag, chol_off, eddy_x, eddy_y, eddy_z, eddy_signs, tile_lists):
    rows, columns = velocity.shape[2:]
    spanwise = columns * lax.axis_size("yz")
    slabs = lax.axis_size("gx")
    plane = velocity[:, 0]
    me = lax.axis_index("gx")
    even = me % 2 == 0
    half = columns // 2
    swap = [(i, i ^ 1) for i in range(slabs)]
    onward = [(i, i + 2) for i in range(slabs - 2)]
    low, high = plane[:, :, :half], plane[:, :, half:]
    keep = jnp.where(even, low, high)
    other = lax.ppermute(jnp.where(even, high, low), "gx", swap)
    near = lax.ppermute(keep, "gx", onward)

    def forward(held):
        return lax.ppermute(held[0], "gx", onward)

    inflow, (other, near), next_near = inlet_planes(
        mean_flow, chol_diag, chol_off, eddy_x, eddy_y, eddy_z, eddy_signs, columns, spanwise, (other, near), forward
    )
    inflow, next_near = lax.optimization_barrier((inflow, next_near))
    p0 = jnp.where(even, keep, other)
    p1 = jnp.where(even, other, keep)
    q0 = jnp.where(even, near, next_near)
    q1 = jnp.where(even, next_near, near)
    chunks = []
    for begin in range(0, half, LANES):
        cut = [value[:, :, begin : begin + LANES] for value in (q0, q1, p0, p1)]
        chunks.append((lax.ppermute(cut[1], "gx", onward), *cut))
    mean_lanes = jnp.broadcast_to(mean_flow[:, None], (rows, LANES))
    level = (me // 2).astype(jnp.int32).reshape(1)
    lows, highs = [], []
    for number, planes in enumerate(chunks):
        begin = number * LANES
        inlet = jnp.where(
            even, inflow[:, :, begin : begin + LANES], inflow[:, :, half + begin : half + begin + LANES]
        ).astype(jnp.bfloat16)
        o0, o1 = march(level, mean_lanes, inlet, *planes)
        keep = jnp.where(even, o0, o1)
        other = lax.ppermute(jnp.where(even, o1, o0), "gx", swap)
        lows.append(jnp.where(even, keep, other))
        highs.append(jnp.where(even, other, keep))
    velocity_next = jnp.concatenate(lows + highs, axis=2)[:, None]
    return (velocity_next, inflow[None])


def solution(mesh):
    placed = (P(None, "gx", None, "yz"), P(), P(), P(), P(), P(), P(), P(), P("yz", None))
    return jax.shard_map(
        body,
        mesh=mesh,
        in_specs=placed,
        out_specs=(P(None, "gx", None, "yz"), P(None, None, None, "yz")),
        check_vma=False,
    )
```

```python
import functools
import math

import jax
import jax.numpy as jnp
import numpy as np
from jax import lax
from jax.experimental import pallas as pl
from jax.experimental.pallas import tpu as pltpu
from jax.sharding import PartitionSpec as P

TILE = 128
EPT = 96
SIGMA = 64
LANES = 128
STRIDE = 128
HALO = 16
WINDOW = STRIDE + 2 * HALO
MESH = pl.DeviceIdType.MESH

shape_peak = math.sqrt(1.5)
time_step = 0.4
viscosity = 0.3
bulk_speed = 1.0


def tent_shape(ratio):
    return shape_peak * jnp.maximum(0.0, 1.0 - jnp.abs(ratio))


def wall_bases(rows):
    inner = 32
    norm = math.sqrt(2.0 / rows)
    y = np.arange(rows)[None, :]
    p = np.arange(rows // inner)[:, None] * inner
    q = np.arange(inner)[:, None]

    def angles(k, position, period):
        return (k * position % period) * (2.0 * math.pi / period)

    def single(table):
        return jnp.asarray(table.astype(np.float32))

    a, b = angles(p, 2 * y + 1, 4 * rows), angles(q, 2 * y + 1, 4 * rows)
    cosine = (
        single(norm * np.cos(a))[:, None] * single(np.cos(b))[None]
        - single(norm * np.sin(a))[:, None] * single(np.sin(b))[None]
    ).reshape(rows, rows)
    cosine = jnp.where(jnp.arange(rows)[:, None] == 0, math.sqrt(1.0 / rows), cosine)
    a, b = angles(p, y + 1, 2 * rows), angles(q, y + 1, 2 * rows)
    sine = (
        single(norm * np.sin(a))[:, None] * single(np.cos(b))[None]
        + single(norm * np.cos(a))[:, None] * single(np.sin(b))[None]
    ).reshape(rows, rows)
    return cosine, sine


def decay_rates(rows):
    return 2.0 * np.arcsinh(np.sin(np.arange(rows) * (math.pi / (2 * rows))))


def line_kernel(f_ref, coef_ref, g_ref, h_ref):
    rate, alpha, beta = coef_ref[0], coef_ref[1], coef_ref[2]
    mean, carry_up, carry_down = coef_ref[3], coef_ref[4], coef_ref[5]
    length = f_ref.shape[0]

    def down(step, carry):
        z = length - 1 - step
        g_ref[z] = carry
        return f_ref[z] - mean + rate * carry

    lax.fori_loop(0, length, down, carry_down, unroll=8)

    def up(z, carry):
        total = f_ref[z] - mean + rate * carry
        after = g_ref[z]
        g_ref[z] = alpha * (total - after)
        h_ref[z] = beta * (total + rate * after)
        return total

    lax.fori_loop(0, length, up, carry_up, unroll=8)


def line_solve(modes, theta, axis, held, forward):
    length, rows = modes.shape
    count = lax.axis_size(axis)
    total = count * length
    me = lax.axis_index(axis)
    short = 32
    outer = np.arange(length // short)[:, None]
    inner = np.arange(short)[:, None]
    blocks = modes.reshape(length // short, short, rows)
    up_out = np.exp(-theta[None] * (length - short - short * outer))
    up_in = np.exp(-theta[None] * (short - 1 - inner))
    down_out = np.exp(-theta[None] * short * outer)
    down_in = np.exp(-theta[None] * inner)
    down_in[:, 0] = inner[:, 0]
    down_out[:, 0] = -1.0
    extra = np.zeros_like(up_out)
    extra[:, 0] = length - short * outer[:, 0]
    table = lambda values: jnp.asarray(values.astype(np.float32))
    part_up = jnp.sum(blocks * table(up_in)[None], axis=1)
    part_down = jnp.sum(blocks * table(down_in)[None], axis=1)
    part_up, part_down, held = lax.optimization_barrier((part_up, part_down, held))
    onward = forward(held)
    sums = jnp.stack(
        [
            jnp.sum(part_up * table(up_out), axis=0),
            jnp.sum(part_down * table(down_out) + part_up * table(extra), axis=0),
        ]
    )
    everyone = lax.all_gather(sums, axis)
    place = jnp.arange(count)
    behind = (me - 1 - place) % count
    ahead = (place - me - 1) % count
    theta_line = jnp.asarray((theta * length).astype(np.float32))
    period = jnp.asarray(np.where(theta > 0, 1.0 / np.maximum(-np.expm1(-theta * total), 1e-30), 1.0).astype(np.float32))
    carry_up = period * jnp.sum(everyone[:, 0] * jnp.exp(-theta_line[None] * behind[:, None].astype(jnp.float32)), axis=0)
    carry_down = period * jnp.sum(everyone[:, 1] * jnp.exp(-theta_line[None] * ahead[:, None].astype(jnp.float32)), axis=0)
    first_tot = everyone[:, 0, 0]
    first_run = everyone[:, 1, 0]
    mean = jnp.sum(first_tot) / total
    tot = first_tot - mean * length
    starts = jnp.cumsum(tot) - tot
    shift = -(jnp.sum(first_run - mean * (length * (length + 1) / 2.0)) + length * jnp.sum(starts)) / total
    mine = (place == me).astype(jnp.float32)
    start = jnp.sum(starts * mine) + shift
    is_first = jnp.arange(rows) == 0
    carry_up = jnp.where(is_first, start, carry_up)
    carry_down = jnp.where(is_first, -start - jnp.sum(tot * mine), carry_down)
    means = jnp.where(is_first, mean, 0.0)
    rate = np.exp(-theta)
    fixed = np.stack([rate, rate / (1.0 + rate), np.sqrt(rate) / (1.0 + rate)]).astype(np.float32)
    coef = jnp.concatenate([jnp.asarray(fixed), jnp.stack([means, carry_up, carry_down])], axis=0)
    coef, onward = lax.optimization_barrier((coef, onward))
    lanes = (rows // LANES, LANES)
    g, h = pl.pallas_call(
        line_kernel,
        out_shape=[jax.ShapeDtypeStruct((length,) + lanes, jnp.float32)] * 2,
        in_specs=[pl.BlockSpec(memory_space=pltpu.VMEM)] * 2,
        out_specs=[pl.BlockSpec(memory_space=pltpu.VMEM)] * 2,
        compiler_params=pltpu.CompilerParams(vmem_limit_bytes=24 * 1024 * 1024),
        cost_estimate=pl.CostEstimate(
            flops=10 * length * rows, bytes_accessed=12 * length * rows, transcendentals=0
        ),
        name="line_solve",
    )(modes.reshape((length,) + lanes), coef.reshape((6,) + lanes))
    return g.reshape(length, rows), h.reshape(length, rows), held, onward


def march_kernel(
    slabs, mean_ref, inlet_ref, keep_ref, other_ref, near_ref, next_ref,
    mine_ref, theirs_ref,
    far, back, far_send, far_recv, back_send, back_recv,
):
    rows = mean_ref.shape[0]
    blocks = rows // STRIDE
    me = lax.axis_index("gx")
    even = me % 2 == 0
    partner = me + 1 - 2 * (me % 2)
    has_after = me + 2 < slabs
    has_before = me >= 2
    after = jnp.where(has_after, me + 2, me - 2)
    at_inlet = me < 2
    after_inlet = (me >= 2) & (me < 4)

    barrier = pltpu.get_barrier_semaphore()
    pl.semaphore_signal(barrier, inc=1, device_id={"gx": partner}, device_id_type=MESH)

    @pl.when(has_after)
    def _():
        pl.semaphore_signal(barrier, inc=1, device_id={"gx": after}, device_id_type=MESH)

    @pl.when(has_before)
    def _():
        pl.semaphore_signal(barrier, inc=1, device_id={"gx": me - 2}, device_id_type=MESH)

    pl.semaphore_wait(barrier, 1 + has_after.astype(jnp.int32) + has_before.astype(jnp.int32))

    def block_rows(block):
        return pl.ds(pl.multiple_of(block * STRIDE, STRIDE), STRIDE)

    def far_copy(source, block):
        return pltpu.make_async_remote_copy(
            src_ref=source.at[:, block_rows(block), :],
            dst_ref=far.at[:, block_rows(block), :],
            send_sem=far_send.at[block],
            recv_sem=far_recv.at[block],
            device_id={"gx": after},
            device_id_type=MESH,
        )

    def back_copy(block):
        return pltpu.make_async_remote_copy(
            src_ref=back.at[:, block_rows(block), :],
            dst_ref=theirs_ref.at[:, block_rows(block), :],
            send_sem=back_send.at[block],
            recv_sem=back_recv.at[block],
            device_id={"gx": partner},
            device_id_type=MESH,
        )

    @pl.when(has_after & even)
    def _():
        @pl.loop(0, blocks)
        def _(block):
            far_copy(next_ref, block).start()

    @pl.when(has_after & (me % 2 == 1))
    def _():
        @pl.loop(0, blocks)
        def _(block):
            far_copy(near_ref, block).start()

    @pl.when(me < 2)
    def _():
        far[...] = jnp.zeros_like(far)

    @pl.when(has_before)
    def _():
        far_copy(near_ref, 0).wait_recv()

    local = lax.broadcasted_iota(jnp.int32, (WINDOW, LANES), 0)

    @pl.loop(0, blocks)
    def _(block):
        @pl.when(has_before & (block + 1 < blocks))
        def _():
            far_copy(near_ref, block + 1).wait_recv()

        start = pl.multiple_of(jnp.clip(block * STRIDE - HALO, 0, rows - WINDOW), HALO)
        here = pl.ds(start, WINDOW)

        @pl.loop(0, keep_ref.shape[2] // LANES)
        def _(column):
            lanes = pl.ds(pl.multiple_of(column * LANES, LANES), LANES)
            low_wall = local + start == 0
            high_wall = local + start == rows - 1
            mean = mean_ref[here, :]
            drag = mean + 2.0 * viscosity

            def load(ref):
                return [ref[c, here, lanes].astype(jnp.float32) for c in range(3)]

            def rate(field, behind):
                half = 0.5 * field[1]
                up, down = viscosity - half, viscosity + half
                out = []
                for c in range(3):
                    above = jnp.where(high_wall, 0.0, jnp.roll(field[c], -1, axis=0))
                    below = jnp.where(low_wall, 0.0, jnp.roll(field[c], 1, axis=0))
                    out.append(up * above + down * below + mean * behind[c] - drag * field[c])
                return out

            def pick(flag, first, second):
                return [jnp.where(flag, a, b) for a, b in zip(first, second)]

            def rounded(field):
                return [a.astype(jnp.bfloat16).astype(jnp.float32) for a in field]

            def one(field, f0):
                return [u + time_step * (8.0 / 15.0) * a for u, a in zip(field, f0)]

            def two(field, f1, f0):
                return [
                    u + (time_step * 5.0 / 12.0) * b - (time_step * 17.0 / 60.0) * a
                    for u, b, a in zip(field, f1, f0)
                ]

            def three(field, f2, f1):
                return [
                    u + (time_step * 0.75) * b - (time_step * 5.0 / 12.0) * a
                    for u, b, a in zip(field, f2, f1)
                ]

            inlet = load(inlet_ref)
            keep, other, near, further = load(keep_ref), load(other_ref), load(near_ref), load(next_ref)
            p0, p1 = pick(even, keep, other), pick(even, other, keep)
            q0, q1 = pick(even, near, further), pick(even, further, near)
            q0_1 = rounded(one(q0, rate(q0, pick(after_inlet, inlet, load(far)))))
            q1_f0 = rate(q1, q0)
            q1_1 = one(q1, q1_f0)
            q1_2 = rounded(two(q1_1, rate(q1_1, q0_1), q1_f0))
            p0_f0 = rate(p0, pick(at_inlet, inlet, q1))
            p0_1 = one(p0, p0_f0)
            p0_f1 = rate(p0_1, pick(at_inlet, inlet, rounded(q1_1)))
            p0_2 = two(p0_1, p0_f1, p0_f0)
            p0_3 = three(p0_2, rate(p0_2, pick(at_inlet, inlet, q1_2)), p0_f1)
            p1_f0 = rate(p1, p0)
            p1_1 = one(p1, p1_f0)
            p1_f1 = rate(p1_1, rounded(p0_1))
            p1_2 = two(p1_1, p1_f1, p1_f0)
            p1_3 = three(p1_2, rate(p1_2, rounded(p0_2)), p1_f1)
            results = ((mine_ref, pick(even, p0_3, p1_3)), (back, pick(even, p1_3, p0_3)))

            def store(skip):
                for ref, value in results:
                    for c in range(3):
                        ref[c, block_rows(block), lanes] = value[c][skip : skip + STRIDE].astype(ref.dtype)

            pl.when(block == 0)(lambda: store(0))
            pl.when((block > 0) & (block < blocks - 1))(lambda: store(HALO))
            pl.when(block == blocks - 1)(lambda: store(2 * HALO))

        back_copy(block).start()

    @pl.loop(0, blocks)
    def _(block):
        back_copy(block).wait_send()
        back_copy(block).wait_recv()

    @pl.when(has_after)
    def _():
        @pl.loop(0, blocks)
        def _(block):
            far_copy(near_ref, block).wait_send()


def march(slabs, mean_lanes, inlet, keep, other, near, next_near):
    shape = keep.shape
    rows = shape[1]
    blocks = rows // STRIDE
    vmem = pl.BlockSpec(memory_space=pltpu.VMEM)
    return pl.pallas_call(
        functools.partial(march_kernel, slabs),
        out_shape=[jax.ShapeDtypeStruct(shape, jnp.bfloat16)] * 2,
        in_specs=[vmem] * 6,
        out_specs=[vmem, pl.BlockSpec(memory_space=pl.ANY)],
        scratch_shapes=[
            pltpu.VMEM(shape, jnp.bfloat16),
            pltpu.VMEM(shape, jnp.bfloat16),
            pltpu.SemaphoreType.DMA((blocks,)),
            pltpu.SemaphoreType.DMA((blocks,)),
            pltpu.SemaphoreType.DMA((blocks,)),
            pltpu.SemaphoreType.DMA((blocks,)),
        ],
        compiler_params=pltpu.CompilerParams(
            collective_id=0, has_side_effects=True, vmem_limit_bytes=36 * 1024 * 1024
        ),
        cost_estimate=pl.CostEstimate(
            flops=324 * math.prod(shape), bytes_accessed=14 * math.prod(shape), transcendentals=0
        ),
        name="march",
    )(mean_lanes, inlet, keep, other, near, next_near)


def inlet_planes(mean_flow, chol_diag, chol_off, eddy_x, eddy_y, eddy_z, eddy_signs, columns, spanwise, held, forward):
    rows = mean_flow.shape[0]
    first_cell = lax.axis_index("yz") * columns
    signs = (2 * eddy_signs - 1).astype(jnp.float32)
    cells_y = jnp.arange(rows, dtype=jnp.int32)
    shape_y = tent_shape((cells_y[None, :] - eddy_y[:, None]).astype(jnp.float32) / SIGMA).astype(jnp.bfloat16)
    amplitude = math.sqrt(8.0 * rows / (TILE * EPT))
    scale = (amplitude * tent_shape(eddy_x.astype(jnp.float32) / SIGMA))[None, :] * signs

    def fluct_at(cells):
        offset = (cells[None, :] - eddy_z[:, None] + spanwise // 2) % spanwise - spanwise // 2
        shape_z = tent_shape(offset.astype(jnp.float32) / SIGMA)
        weight = (scale[:, :, None] * shape_z[None]).astype(jnp.bfloat16)
        return jnp.einsum("ey,jez->jyz", shape_y, weight, preferred_element_type=jnp.float32)

    fluct = fluct_at(first_cell + jnp.arange(columns, dtype=jnp.int32))
    edge = fluct_at((first_cell - 1 + spanwise) % spanwise + jnp.arange(1, dtype=jnp.int32))

    def mix(fl):
        return chol_off[1][:, None] * fl[0] + chol_off[2][:, None] * fl[1] + chol_diag[2][:, None] * fl[2]

    first = mean_flow[:, None] + chol_diag[0][:, None] * fluct[0]
    second = chol_off[0][:, None] * fluct[0] + chol_diag[1][:, None] * fluct[1]
    third = mix(fluct)
    flux = second * (cells_y < rows - 1).astype(jnp.float32)[:, None]
    lower = jnp.concatenate([jnp.zeros_like(flux[:1]), flux[:-1]], axis=0)
    previous = jnp.concatenate([mix(edge), third[:, :-1]], axis=1)
    div = flux - lower + third - previous
    high = lax.Precision.HIGH
    cosine, sine = wall_bases(rows)
    modes = jnp.einsum("yz,ky->zk", div, cosine, precision=high)
    slope_modes, rise_modes, held, onward = line_solve(modes, decay_rates(rows), "yz", held, forward)
    slope = jnp.einsum(
        "ky,zk->yz", cosine.astype(jnp.bfloat16), slope_modes.astype(jnp.bfloat16), preferred_element_type=jnp.float32
    )
    rise = jnp.einsum(
        "ky,zk->yz", sine.astype(jnp.bfloat16), rise_modes.astype(jnp.bfloat16), preferred_element_type=jnp.float32
    )
    return jnp.stack([first, flux - rise, third - slope], axis=0), held, onward


def body(velocity, mean_flow, chol_diag, chol_off, eddy_x, eddy_y, eddy_z, eddy_signs, tile_lists):
    rows, columns = velocity.shape[2:]
    spanwise = columns * lax.axis_size("yz")
    slabs = lax.axis_size("gx")
    plane = velocity[:, 0]
    me = lax.axis_index("gx")
    even = me % 2 == 0
    half = columns // 2
    swap = [(i, i ^ 1) for i in range(slabs)]
    onward = [(i, i + 2) for i in range(slabs - 2)]
    low, high = plane[:, :, :half], plane[:, :, half:]
    keep = jnp.where(even, low, high)
    other = lax.ppermute(jnp.where(even, high, low), "gx", swap)
    near = lax.ppermute(keep, "gx", onward)

    def forward(held):
        return lax.ppermute(held[0], "gx", onward)

    inflow, (other, near), next_near = inlet_planes(
        mean_flow, chol_diag, chol_off, eddy_x, eddy_y, eddy_z, eddy_signs, columns, spanwise, (other, near), forward
    )
    inlet = jnp.where(even, inflow[:, :, :half], inflow[:, :, half:]).astype(jnp.bfloat16)
    mean_lanes = jnp.broadcast_to(mean_flow[:, None], (rows, LANES))
    mine, theirs = march(slabs, mean_lanes, inlet, keep, other, near, next_near)
    velocity_next = jnp.concatenate(
        [jnp.where(even, mine, theirs), jnp.where(even, theirs, mine)], axis=2
    )[:, None]
    return (velocity_next, inflow[None])


def solution(mesh):
    placed = (P(None, "gx", None, "yz"), P(), P(), P(), P(), P(), P(), P(), P("yz", None))
    return jax.shard_map(
        body,
        mesh=mesh,
        in_specs=placed,
        out_specs=(P(None, "gx", None, "yz"), P(None, None, None, "yz")),
        check_vma=False,
    )
```

```python
import functools
import math

import jax
import jax.numpy as jnp
import numpy as np
from jax import lax
from jax.experimental import pallas as pl
from jax.experimental.pallas import tpu as pltpu
from jax.sharding import PartitionSpec as P

TILE = 128
EPT = 96
SIGMA = 64
LANES = 128
STRIDE = 128
HALO = 16
WINDOW = STRIDE + 2 * HALO
MESH = pl.DeviceIdType.MESH

shape_peak = math.sqrt(1.5)
time_step = 0.4
viscosity = 0.3
bulk_speed = 1.0


def tent_shape(ratio):
    return shape_peak * jnp.maximum(0.0, 1.0 - jnp.abs(ratio))


def wall_bases(rows):
    inner = 32
    norm = math.sqrt(2.0 / rows)
    y = np.arange(rows)[None, :]
    p = np.arange(rows // inner)[:, None] * inner
    q = np.arange(inner)[:, None]

    def angles(k, position, period):
        return (k * position % period) * (2.0 * math.pi / period)

    def single(table):
        return jnp.asarray(table.astype(np.float32))

    a, b = angles(p, 2 * y + 1, 4 * rows), angles(q, 2 * y + 1, 4 * rows)
    cosine = (
        single(norm * np.cos(a))[:, None] * single(np.cos(b))[None]
        - single(norm * np.sin(a))[:, None] * single(np.sin(b))[None]
    ).reshape(rows, rows)
    cosine = jnp.where(jnp.arange(rows)[:, None] == 0, math.sqrt(1.0 / rows), cosine)
    a, b = angles(p, y + 1, 2 * rows), angles(q, y + 1, 2 * rows)
    sine = (
        single(norm * np.sin(a))[:, None] * single(np.cos(b))[None]
        + single(norm * np.cos(a))[:, None] * single(np.sin(b))[None]
    ).reshape(rows, rows)
    return cosine, sine


def decay_rates(rows):
    return 2.0 * np.arcsinh(np.sin(np.arange(rows) * (math.pi / (2 * rows))))


def line_kernel(f_ref, coef_ref, g_ref, h_ref):
    rate, alpha, beta = coef_ref[0], coef_ref[1], coef_ref[2]
    mean, carry_up, carry_down = coef_ref[3], coef_ref[4], coef_ref[5]
    length = f_ref.shape[0]

    def down(step, carry):
        z = length - 1 - step
        g_ref[z] = carry
        return f_ref[z] - mean + rate * carry

    lax.fori_loop(0, length, down, carry_down, unroll=8)

    def up(z, carry):
        total = f_ref[z] - mean + rate * carry
        after = g_ref[z]
        g_ref[z] = alpha * (total - after)
        h_ref[z] = beta * (total + rate * after)
        return total

    lax.fori_loop(0, length, up, carry_up, unroll=8)


def line_solve(modes, theta, axis, held, forward):
    length, rows = modes.shape
    count = lax.axis_size(axis)
    total = count * length
    me = lax.axis_index(axis)
    short = 32
    outer = np.arange(length // short)[:, None]
    inner = np.arange(short)[:, None]
    blocks = modes.reshape(length // short, short, rows)
    up_out = np.exp(-theta[None] * (length - short - short * outer))
    up_in = np.exp(-theta[None] * (short - 1 - inner))
    down_out = np.exp(-theta[None] * short * outer)
    down_in = np.exp(-theta[None] * inner)
    down_in[:, 0] = inner[:, 0]
    down_out[:, 0] = -1.0
    extra = np.zeros_like(up_out)
    extra[:, 0] = length - short * outer[:, 0]
    table = lambda values: jnp.asarray(values.astype(np.float32))
    part_up = jnp.sum(blocks * table(up_in)[None], axis=1)
    part_down = jnp.sum(blocks * table(down_in)[None], axis=1)
    part_up, part_down, held = lax.optimization_barrier((part_up, part_down, held))
    onward = forward(held)
    sums = jnp.stack(
        [
            jnp.sum(part_up * table(up_out), axis=0),
            jnp.sum(part_down * table(down_out) + part_up * table(extra), axis=0),
        ]
    )
    everyone = lax.all_gather(sums, axis)
    everyone, early = lax.optimization_barrier((everyone, onward[0]))
    onward = (early, onward[1])
    place = jnp.arange(count)
    behind = (me - 1 - place) % count
    ahead = (place - me - 1) % count
    theta_line = jnp.asarray((theta * length).astype(np.float32))
    period = jnp.asarray(np.where(theta > 0, 1.0 / np.maximum(-np.expm1(-theta * total), 1e-30), 1.0).astype(np.float32))
    carry_up = period * jnp.sum(everyone[:, 0] * jnp.exp(-theta_line[None] * behind[:, None].astype(jnp.float32)), axis=0)
    carry_down = period * jnp.sum(everyone[:, 1] * jnp.exp(-theta_line[None] * ahead[:, None].astype(jnp.float32)), axis=0)
    first_tot = everyone[:, 0, 0]
    first_run = everyone[:, 1, 0]
    mean = jnp.sum(first_tot) / total
    tot = first_tot - mean * length
    starts = jnp.cumsum(tot) - tot
    shift = -(jnp.sum(first_run - mean * (length * (length + 1) / 2.0)) + length * jnp.sum(starts)) / total
    mine = (place == me).astype(jnp.float32)
    start = jnp.sum(starts * mine) + shift
    is_first = jnp.arange(rows) == 0
    carry_up = jnp.where(is_first, start, carry_up)
    carry_down = jnp.where(is_first, -start - jnp.sum(tot * mine), carry_down)
    means = jnp.where(is_first, mean, 0.0)
    rate = np.exp(-theta)
    fixed = np.stack([rate, rate / (1.0 + rate), np.sqrt(rate) / (1.0 + rate)]).astype(np.float32)
    coef = jnp.concatenate([jnp.asarray(fixed), jnp.stack([means, carry_up, carry_down])], axis=0)
    lanes = (rows // LANES, LANES)
    g, h = pl.pallas_call(
        line_kernel,
        out_shape=[jax.ShapeDtypeStruct((length,) + lanes, jnp.float32)] * 2,
        in_specs=[pl.BlockSpec(memory_space=pltpu.VMEM)] * 2,
        out_specs=[pl.BlockSpec(memory_space=pltpu.VMEM)] * 2,
        compiler_params=pltpu.CompilerParams(vmem_limit_bytes=24 * 1024 * 1024),
        cost_estimate=pl.CostEstimate(
            flops=length * rows, bytes_accessed=length * rows, transcendentals=0
        ),
        name="line_solve",
    )(modes.reshape((length,) + lanes), coef.reshape((6,) + lanes))
    return g.reshape(length, rows), h.reshape(length, rows), held, onward


def march_kernel(
    slabs, mean_ref, inlet_ref, keep_ref, other_ref, near_ref, next_ref,
    mine_ref, theirs_ref,
    far, back, far_send, far_recv, back_send, back_recv,
):
    rows = mean_ref.shape[0]
    blocks = rows // STRIDE
    me = lax.axis_index("gx")
    even = me % 2 == 0
    partner = me + 1 - 2 * (me % 2)
    has_after = me + 2 < slabs
    has_before = me >= 2
    after = jnp.where(has_after, me + 2, me - 2)
    at_inlet = me < 2
    after_inlet = (me >= 2) & (me < 4)

    barrier = pltpu.get_barrier_semaphore()
    pl.semaphore_signal(barrier, inc=1, device_id={"gx": partner}, device_id_type=MESH)

    @pl.when(has_after)
    def _():
        pl.semaphore_signal(barrier, inc=1, device_id={"gx": after}, device_id_type=MESH)

    @pl.when(has_before)
    def _():
        pl.semaphore_signal(barrier, inc=1, device_id={"gx": me - 2}, device_id_type=MESH)

    pl.semaphore_wait(barrier, 1 + has_after.astype(jnp.int32) + has_before.astype(jnp.int32))

    def block_rows(block):
        return pl.ds(pl.multiple_of(block * STRIDE, STRIDE), STRIDE)

    def far_copy(source, block):
        return pltpu.make_async_remote_copy(
            src_ref=source.at[:, block_rows(block), :],
            dst_ref=far.at[:, block_rows(block), :],
            send_sem=far_send.at[block],
            recv_sem=far_recv.at[block],
            device_id={"gx": after},
            device_id_type=MESH,
        )

    def back_copy(block):
        return pltpu.make_async_remote_copy(
            src_ref=back.at[:, block_rows(block), :],
            dst_ref=theirs_ref.at[:, block_rows(block), :],
            send_sem=back_send.at[block],
            recv_sem=back_recv.at[block],
            device_id={"gx": partner},
            device_id_type=MESH,
        )

    @pl.when(has_after & even)
    def _():
        @pl.loop(0, blocks)
        def _(block):
            far_copy(next_ref, block).start()

    @pl.when(has_after & (me % 2 == 1))
    def _():
        @pl.loop(0, blocks)
        def _(block):
            far_copy(near_ref, block).start()

    @pl.when(me < 2)
    def _():
        far[...] = jnp.zeros_like(far)

    @pl.when(has_before)
    def _():
        far_copy(near_ref, 0).wait_recv()

    local = lax.broadcasted_iota(jnp.int32, (WINDOW, LANES), 0)

    @pl.loop(0, blocks)
    def _(block):
        @pl.when(has_before & (block + 1 < blocks))
        def _():
            far_copy(near_ref, block + 1).wait_recv()

        start = pl.multiple_of(jnp.clip(block * STRIDE - HALO, 0, rows - WINDOW), HALO)
        here = pl.ds(start, WINDOW)

        @pl.loop(0, keep_ref.shape[2] // LANES)
        def _(column):
            lanes = pl.ds(pl.multiple_of(column * LANES, LANES), LANES)
            low_wall = local + start == 0
            high_wall = local + start == rows - 1
            mean = mean_ref[here, :]
            drag = mean + 2.0 * viscosity

            def load(ref):
                return [ref[c, here, lanes].astype(jnp.float32) for c in range(3)]

            def rate(field, behind):
                half = 0.5 * field[1]
                up, down = viscosity - half, viscosity + half
                out = []
                for c in range(3):
                    above = jnp.where(high_wall, 0.0, jnp.roll(field[c], -1, axis=0))
                    below = jnp.where(low_wall, 0.0, jnp.roll(field[c], 1, axis=0))
                    out.append(up * above + down * below + mean * behind[c] - drag * field[c])
                return out

            def pick(flag, first, second):
                return [jnp.where(flag, a, b) for a, b in zip(first, second)]

            def rounded(field):
                return [a.astype(jnp.bfloat16).astype(jnp.float32) for a in field]

            def one(field, f0):
                return [u + time_step * (8.0 / 15.0) * a for u, a in zip(field, f0)]

            def two(field, f1, f0):
                return [
                    u + (time_step * 5.0 / 12.0) * b - (time_step * 17.0 / 60.0) * a
                    for u, b, a in zip(field, f1, f0)
                ]

            def three(field, f2, f1):
                return [
                    u + (time_step * 0.75) * b - (time_step * 5.0 / 12.0) * a
                    for u, b, a in zip(field, f2, f1)
                ]

            inlet = load(inlet_ref)
            keep, other, near, further = load(keep_ref), load(other_ref), load(near_ref), load(next_ref)
            p0, p1 = pick(even, keep, other), pick(even, other, keep)
            q0, q1 = pick(even, near, further), pick(even, further, near)
            q0_1 = rounded(one(q0, rate(q0, pick(after_inlet, inlet, load(far)))))
            q1_f0 = rate(q1, q0)
            q1_1 = one(q1, q1_f0)
            q1_2 = rounded(two(q1_1, rate(q1_1, q0_1), q1_f0))
            p0_f0 = rate(p0, pick(at_inlet, inlet, q1))
            p0_1 = one(p0, p0_f0)
            p0_f1 = rate(p0_1, pick(at_inlet, inlet, rounded(q1_1)))
            p0_2 = two(p0_1, p0_f1, p0_f0)
            p0_3 = three(p0_2, rate(p0_2, pick(at_inlet, inlet, q1_2)), p0_f1)
            p1_f0 = rate(p1, p0)
            p1_1 = one(p1, p1_f0)
            p1_f1 = rate(p1_1, rounded(p0_1))
            p1_2 = two(p1_1, p1_f1, p1_f0)
            p1_3 = three(p1_2, rate(p1_2, rounded(p0_2)), p1_f1)
            results = ((mine_ref, pick(even, p0_3, p1_3)), (back, pick(even, p1_3, p0_3)))

            def store(skip):
                for ref, value in results:
                    for c in range(3):
                        ref[c, block_rows(block), lanes] = value[c][skip : skip + STRIDE].astype(ref.dtype)

            pl.when(block == 0)(lambda: store(0))
            pl.when((block > 0) & (block < blocks - 1))(lambda: store(HALO))
            pl.when(block == blocks - 1)(lambda: store(2 * HALO))

        back_copy(block).start()

    @pl.loop(0, blocks)
    def _(block):
        back_copy(block).wait_send()
        back_copy(block).wait_recv()

    @pl.when(has_after)
    def _():
        @pl.loop(0, blocks)
        def _(block):
            far_copy(near_ref, block).wait_send()


def march(slabs, mean_lanes, inlet, keep, other, near, next_near):
    shape = keep.shape
    rows = shape[1]
    blocks = rows // STRIDE
    vmem = pl.BlockSpec(memory_space=pltpu.VMEM)
    return pl.pallas_call(
        functools.partial(march_kernel, slabs),
        out_shape=[jax.ShapeDtypeStruct(shape, jnp.bfloat16)] * 2,
        in_specs=[vmem] * 6,
        out_specs=[vmem, pl.BlockSpec(memory_space=pl.ANY)],
        scratch_shapes=[
            pltpu.VMEM(shape, jnp.bfloat16),
            pltpu.VMEM(shape, jnp.bfloat16),
            pltpu.SemaphoreType.DMA((blocks,)),
            pltpu.SemaphoreType.DMA((blocks,)),
            pltpu.SemaphoreType.DMA((blocks,)),
            pltpu.SemaphoreType.DMA((blocks,)),
        ],
        compiler_params=pltpu.CompilerParams(
            collective_id=0, has_side_effects=True, vmem_limit_bytes=36 * 1024 * 1024
        ),
        cost_estimate=pl.CostEstimate(
            flops=324 * math.prod(shape), bytes_accessed=14 * math.prod(shape), transcendentals=0
        ),
        name="march",
    )(mean_lanes, inlet, keep, other, near, next_near)


def inlet_planes(mean_flow, chol_diag, chol_off, eddy_x, eddy_y, eddy_z, eddy_signs, columns, spanwise, held, forward):
    rows = mean_flow.shape[0]
    first_cell = lax.axis_index("yz") * columns
    signs = (2 * eddy_signs - 1).astype(jnp.float32)
    cells_y = jnp.arange(rows, dtype=jnp.int32)
    shape_y = tent_shape((cells_y[None, :] - eddy_y[:, None]).astype(jnp.float32) / SIGMA).astype(jnp.bfloat16)
    amplitude = math.sqrt(8.0 * rows / (TILE * EPT))
    scale = (amplitude * tent_shape(eddy_x.astype(jnp.float32) / SIGMA))[None, :] * signs

    def fluct_at(cells):
        offset = (cells[None, :] - eddy_z[:, None] + spanwise // 2) % spanwise - spanwise // 2
        shape_z = tent_shape(offset.astype(jnp.float32) / SIGMA)
        weight = (scale[:, :, None] * shape_z[None]).astype(jnp.bfloat16)
        return jnp.einsum("ey,jez->jyz", shape_y, weight, preferred_element_type=jnp.float32)

    fluct = fluct_at(first_cell + jnp.arange(columns, dtype=jnp.int32))
    edge = fluct_at((first_cell - 1 + spanwise) % spanwise + jnp.arange(1, dtype=jnp.int32))

    def mix(fl):
        return chol_off[1][:, None] * fl[0] + chol_off[2][:, None] * fl[1] + chol_diag[2][:, None] * fl[2]

    first = mean_flow[:, None] + chol_diag[0][:, None] * fluct[0]
    second = chol_off[0][:, None] * fluct[0] + chol_diag[1][:, None] * fluct[1]
    third = mix(fluct)
    flux = second * (cells_y < rows - 1).astype(jnp.float32)[:, None]
    lower = jnp.concatenate([jnp.zeros_like(flux[:1]), flux[:-1]], axis=0)
    previous = jnp.concatenate([mix(edge), third[:, :-1]], axis=1)
    div = flux - lower + third - previous
    high = lax.Precision.HIGH
    cosine, sine = wall_bases(rows)
    modes = jnp.einsum("yz,ky->zk", div, cosine, precision=high)
    slope_modes, rise_modes, held, onward = line_solve(modes, decay_rates(rows), "yz", held, forward)
    slope = jnp.einsum(
        "ky,zk->yz", cosine.astype(jnp.bfloat16), slope_modes.astype(jnp.bfloat16), preferred_element_type=jnp.float32
    )
    rise = jnp.einsum(
        "ky,zk->yz", sine.astype(jnp.bfloat16), rise_modes.astype(jnp.bfloat16), preferred_element_type=jnp.float32
    )
    second, third, late = lax.optimization_barrier((flux - rise, third - slope, onward[1]))
    onward = jnp.concatenate([onward[0], late], axis=1)
    return jnp.stack([first, second, third], axis=0), held, onward


def body(velocity, mean_flow, chol_diag, chol_off, eddy_x, eddy_y, eddy_z, eddy_signs, tile_lists):
    rows, columns = velocity.shape[2:]
    spanwise = columns * lax.axis_size("yz")
    slabs = lax.axis_size("gx")
    plane = velocity[:, 0]
    me = lax.axis_index("gx")
    even = me % 2 == 0
    half = columns // 2
    swap = [(i, i ^ 1) for i in range(slabs)]
    onward = [(i, i + 2) for i in range(slabs - 2)]
    low, high = plane[:, :, :half], plane[:, :, half:]
    keep = jnp.where(even, low, high)
    other = lax.ppermute(jnp.where(even, high, low), "gx", swap)
    near = lax.ppermute(keep, "gx", onward)

    def forward(held):
        middle = rows // 2
        return tuple(lax.ppermute(part, "gx", onward) for part in (held[0][:, :middle], held[0][:, middle:]))

    inflow, (other, near), next_near = inlet_planes(
        mean_flow, chol_diag, chol_off, eddy_x, eddy_y, eddy_z, eddy_signs, columns, spanwise, (other, near), forward
    )
    inlet = jnp.where(even, inflow[:, :, :half], inflow[:, :, half:]).astype(jnp.bfloat16)
    mean_lanes = jnp.broadcast_to(mean_flow[:, None], (rows, LANES))
    mine, theirs = march(slabs, mean_lanes, inlet, keep, other, near, next_near)
    velocity_next = jnp.concatenate(
        [jnp.where(even, mine, theirs), jnp.where(even, theirs, mine)], axis=2
    )[:, None]
    return (velocity_next, inflow[None])


def solution(mesh):
    placed = (P(None, "gx", None, "yz"), P(), P(), P(), P(), P(), P(), P(), P("yz", None))
    return jax.shard_map(
        body,
        mesh=mesh,
        in_specs=placed,
        out_specs=(P(None, "gx", None, "yz"), P(None, None, None, "yz")),
        check_vma=False,
    )
```
